32 devices in a mesh: row: 8 (over y, x, core), col: 4 (over z).
Axes of the slice: x: 2, y: 2, z: 4, core: 2. Of those that a mesh axis runs over, the one named last changes fastest.
Arguments:
- panel_tiles: float32 [16384, 1024], P('row', 'col'), may hold values from -48 to 48
- left_u: bfloat16 [16384, 6144], P('row', 'col'), may hold values from -8 to 8
- earlier_right_factors: bfloat16 [16384, 6144], P('row', 'col'), may hold values from -0.25 to 0.25
- tile_global_index: int32 [16], replicated, may hold values from 0 to 15, as said below
Outputs:
- panel_factor: float32 [16384, 1024], P('row', 'col')
The draws below stay inside these ranges and needn't reach their ends.
Inputs may be any that keep to these rules, and one draw needn't show every extreme that they name: `tile_global_index`: A permutation; slot pivot, the one numbered 0, holds the diagonal tile.
All inputs are finite; a program needn't handle non-finite values.
Results may differ from the reference program's by a relative error of at most 0.00053.
Values may be sent and summed in bfloat16 or wider, within the bound.
A program may use at most 128 MiB of HBM per device.

```python
import math
import jax
import jax.numpy as jnp
from jax import lax

TILE = 1024
RANK = 256
TILES = 16
COLS = 24


kernel_height = 30.0


nugget_level = 16.0


factor_bound = 0.25


def pivot_draw(key):
    ordering = jax.random.permutation(jax.random.fold_in(key, 11), TILES).astype(jnp.int32)
    pivot_position = jnp.sum(jnp.where(ordering == 0, jnp.arange(TILES, dtype=jnp.int32), 0)).astype(jnp.int32)
    return (ordering, pivot_position)


def update_scale():
    aspect_ratio = TILE / (COLS * RANK)
    edge_factor = (1.0 + math.sqrt(aspect_ratio)) ** 2 * (1.0 + 0.5 * RANK / TILE)
    margin_factor = 1.05 + 1.5 / math.sqrt(TILE)
    return math.sqrt(nugget_level / (edge_factor * margin_factor * COLS * RANK))


def draw_tile_global_index(key, part):
    ordering, pivot_position = pivot_draw(key)
    return ordering


def draw_panel_tiles(key, part):
    ordering, pivot_position = pivot_draw(key)
    background = jnp.clip(jax.random.normal(jax.random.fold_in(key, 21), (TILES * TILE, TILE), jnp.float32), -6.0, 6.0) * 0.5
    length_scale = 0.15
    points = jax.random.uniform(jax.random.fold_in(key, 24), (TILE, 2), jnp.float32)
    offsets = points[:, None, :] - points[None, :, :]
    distance = jnp.sqrt(jnp.sum(offsets * offsets, axis=2))
    pivot_block = kernel_height * jnp.exp(-distance / length_scale) + nugget_level * jnp.eye(TILE, dtype=jnp.float32)
    start_row = (pivot_position * TILE).astype(jnp.int32)
    result = lax.dynamic_update_slice(background, pivot_block, (start_row, jnp.int32(0)))
    return result.astype(jnp.float32)


def draw_left_u(key, part):
    ordering, pivot_position = pivot_draw(key)
    background = jnp.clip(jax.random.normal(jax.random.fold_in(key, 31), (TILES * TILE, COLS * RANK), jnp.float32), -6.0, 6.0) * 0.3
    pivot_rows = jnp.clip(jax.random.normal(jax.random.fold_in(key, 32), (TILE, COLS * RANK), jnp.float32), -6.0, 6.0) * update_scale()
    start_row = (pivot_position * TILE).astype(jnp.int32)
    result = lax.dynamic_update_slice(background, pivot_rows, (start_row, jnp.int32(0)))
    return result.astype(jnp.bfloat16)


def draw_earlier_right_factors(key, part):
    normal_draw = jnp.clip(jax.random.normal(jax.random.fold_in(key, 41), (TILES * TILE, COLS * RANK), jnp.float32), -6.0, 6.0)
    scaled = jnp.clip(normal_draw * (1.0 / math.sqrt(TILE)), -factor_bound, factor_bound)
    return scaled.astype(jnp.bfloat16)


def setup_inputs(seed: int = 0) -> dict:
    seeds = jax.random.split(jax.random.key(seed), 5)
    return {
        "panel_tiles": draw_panel_tiles(jax.random.fold_in(seeds[4], 71), 0),
        "left_u": draw_left_u(jax.random.fold_in(seeds[4], 71), 0),
        "earlier_right_factors": draw_earlier_right_factors(jax.random.fold_in(seeds[4], 71), 0),
        "tile_global_index": draw_tile_global_index(jax.random.fold_in(seeds[4], 71), 0),
    }


def reference(panel_tiles, left_u, earlier_right_factors, tile_global_index):
    pivot_position = jnp.sum(jnp.where(tile_global_index == 0, jnp.arange(TILES, dtype=jnp.int32), 0)).astype(jnp.int32)
    first_row = (pivot_position * TILE).astype(jnp.int32)
    pivot_left = lax.dynamic_slice_in_dim(left_u, first_row, TILE, 0)
    pivot_right = lax.dynamic_slice_in_dim(earlier_right_factors, first_row, TILE, 0)
    pivot_triple = pivot_right.astype(jnp.float32).reshape(TILE, COLS, RANK)

    def tile_update(factors):
        u_rows, v_rows = factors
        inner_small = jnp.einsum('bjr,bjs->jrs', v_rows.astype(jnp.float32).reshape(TILE, COLS, RANK), pivot_triple).astype(jnp.bfloat16)
        left_small = jnp.einsum('bjr,jrs->bjs', u_rows.astype(jnp.float32).reshape(TILE, COLS, RANK), inner_small.astype(jnp.float32)).astype(jnp.bfloat16)
        return jnp.dot(left_small.reshape(TILE, COLS * RANK).astype(jnp.float32), pivot_left.T.astype(jnp.float32), preferred_element_type=jnp.float32)
    update_terms = lax.map(tile_update, (left_u.reshape(TILES, TILE, COLS * RANK), earlier_right_factors.reshape(TILES, TILE, COLS * RANK)))
    updated_tiles = panel_tiles.reshape(TILES, TILE, TILE) - update_terms
    diagonal = lax.dynamic_index_in_dim(updated_tiles, pivot_position, 0, keepdims=False)
    cholesky_factor = jnp.linalg.cholesky(diagonal)
    identity = jnp.eye(TILE, dtype=jnp.float32)
    inverted_factor = lax.linalg.triangular_solve(cholesky_factor, identity, left_side=True, lower=True)
    solved_rows = jnp.einsum('fvk,ik->fvi', updated_tiles, inverted_factor, precision=lax.Precision.HIGHEST)
    chosen = (jnp.arange(TILES, dtype=jnp.int32) == pivot_position)[:, None, None]
    result = jnp.where(chosen, cholesky_factor[None, :, :], solved_rows)
    return result.reshape(TILES * TILE, TILE)
```

```python
import functools

import jax
import jax.numpy as jnp
from jax import lax
from jax.experimental import pallas as pl
from jax.experimental.pallas import tpu as pltpu
from jax.sharding import PartitionSpec as P

TILE = 1024
RANK = 256

BLK = 128
SUB = 8
F32 = jnp.float32
HI = lax.Precision.HIGHEST


def dot(a, b, dims=((1,), (0,))):
    return lax.dot_general(a, b, (dims, ((), ())), precision=HI, preferred_element_type=F32)


def eliminate(block):
    shape = (SUB, BLK)
    groups = [block[g * SUB:(g + 1) * SUB, :] for g in range(BLK // SUB)]
    lane = lax.broadcasted_iota(jnp.int32, shape, 1)
    sub = lax.broadcasted_iota(jnp.int32, shape, 0)
    for g in range(len(groups)):
        base = g * SUB
        rows = groups[g]
        cols = [jnp.broadcast_to(rows[:, base + j:base + j + 1], shape) for j in range(SUB)]
        out = rows
        for s in range(SUB):
            raw = jnp.broadcast_to(rows[s:s + 1, :], shape)
            here = lane == base + s
            mine = sub == s
            out = jnp.where(mine, raw, out)
            inverse = 1.0 / jnp.broadcast_to(cols[s][s:s + 1, :], shape)
            factor = jnp.where(mine, 0.0, cols[s] * inverse)
            unit = jnp.where(here, 1.0, raw)
            kept = jnp.where(here, 0.0, rows)
            rows = jnp.where(mine, unit * inverse, kept - factor * unit)
            for j in range(s + 1, SUB):
                head = jnp.broadcast_to(cols[j][s:s + 1, :], shape)
                cols[j] = jnp.where(mine, head * inverse, cols[j] - factor * head)
        groups[g] = out
        if g + 1 == len(groups):
            break
        reduced = [jnp.broadcast_to(rows[s:s + 1, :], shape) for s in range(SUB)]
        inside = jnp.logical_and(lane >= base, lane < base + SUB)
        for h in range(g + 1, len(groups)):
            old = groups[h]
            terms = [
                jnp.broadcast_to(old[:, base + s:base + s + 1], shape) * reduced[s] for s in range(SUB)
            ]
            while len(terms) > 1:
                terms = [terms[i] + terms[i + 1] for i in range(0, len(terms), 2)]
            groups[h] = jnp.where(inside, 0.0, old) - terms[0]
    return jnp.concatenate(groups, axis=0)


def factor_kernel(a_ref, l_ref, x_ref, w_ref):
    size = a_ref.shape[0]
    count = size // BLK
    row_id = lax.broadcasted_iota(jnp.int32, (BLK, BLK), 0)
    col_id = lax.broadcasted_iota(jnp.int32, (BLK, BLK), 1)

    @pl.loop(0, count)
    def _(i):
        at = pl.ds(pl.multiple_of(i * BLK, BLK), BLK)
        w_ref[at, :] = a_ref[at, :]
        l_ref[at, :] = jnp.zeros((BLK, size), F32)

    @pl.loop(0, count)
    def _(k):
        at = pl.ds(pl.multiple_of(k * BLK, BLK), BLK)
        done = eliminate(w_ref[at, at])
        pivots = jnp.sum(jnp.where(row_id == col_id, done, 0.0), axis=1, keepdims=True)
        scale = 1.0 / jnp.sqrt(pivots)
        upper = jnp.where(col_id >= row_id, done * scale, 0.0)
        inner = jnp.where(col_id < row_id, done * scale, 0.0) + jnp.where(row_id == col_id, scale, 0.0)
        l_ref[at, at] = upper.T
        row = dot(inner, w_ref[at, :])
        block_id = lax.broadcasted_iota(jnp.int32, (BLK, size), 1) // BLK
        row = jnp.where(block_id == k, jnp.concatenate([inner] * count, axis=1), row)
        x_ref[at, :] = jnp.where(block_id <= k, row, 0.0)
        inner_t = inner.T

        @pl.loop(k + 1, count)
        def _(i):
            there = pl.ds(pl.multiple_of(i * BLK, BLK), BLK)
            left = dot(w_ref[there, at], inner_t)
            l_ref[there, at] = left
            w_ref[there, at] = jnp.zeros((BLK, BLK), F32)
            w_ref[there, :] = w_ref[there, :] - dot(left, row)


def factor(a):
    size = a.shape[0]
    shape = jax.ShapeDtypeStruct((size, size), F32)
    return pl.pallas_call(
        factor_kernel,
        out_shape=(shape, shape),
        in_specs=[pl.BlockSpec(memory_space=pltpu.VMEM)],
        out_specs=(pl.BlockSpec(memory_space=pltpu.VMEM),) * 2,
        scratch_shapes=[pltpu.VMEM((size, size), F32)],
        compiler_params=pltpu.CompilerParams(vmem_limit_bytes=32 * 1024 * 1024),
        cost_estimate=pl.CostEstimate(flops=60_000_000_000, bytes_accessed=3 * size * size * 4, transcendentals=0),
        name="factor",
    )(a)


def left_kernel(v_ref, pivot_ref, u_ref, out_ref):
    inner = lax.dot_general(
        v_ref[...], pivot_ref[...], (((0,), (0,)), ((), ())), preferred_element_type=F32
    ).astype(jnp.bfloat16)
    out_ref[...] = jnp.dot(u_ref[...], inner, preferred_element_type=F32).astype(jnp.bfloat16)


def left_factors(v, pivot_v, u):
    slots = v.shape[0] // TILE
    rows = u.shape[0] // slots
    return pl.pallas_call(
        left_kernel,
        grid=(v.shape[1] // RANK, slots),
        out_shape=jax.ShapeDtypeStruct(u.shape, jnp.bfloat16),
        in_specs=[
            pl.BlockSpec((TILE, RANK), lambda j, t: (t, j)),
            pl.BlockSpec((TILE, RANK), lambda j, t: (0, j)),
            pl.BlockSpec((rows, RANK), lambda j, t: (t, j)),
        ],
        out_specs=pl.BlockSpec((rows, RANK), lambda j, t: (t, j)),
        cost_estimate=pl.CostEstimate(
            flops=2 * v.size * RANK + 2 * u.size * RANK,
            bytes_accessed=2 * (v.size + 2 * u.size + pivot_v.size),
            transcendentals=0,
        ),
        name="left",
    )(v, pivot_v, u)


def place(block, width, start):
    return lax.dynamic_update_slice_in_dim(jnp.zeros((block.shape[0], width), block.dtype), block, start, 1)


def local(mesh, panel_tiles, left_u, earlier_right_factors, tile_global_index):
    row_devices = mesh.shape["row"]
    tile_count = tile_global_index.shape[0]
    rows, col_width = panel_tiles.shape
    slots = rows // TILE
    pivot_position = jnp.sum(
        jnp.where(tile_global_index == 0, jnp.arange(tile_count, dtype=jnp.int32), 0)
    )
    owner_row = pivot_position // slots
    local_slot = pivot_position % slots
    my_row = lax.axis_index("row")
    my_col = lax.axis_index("col")
    mine = my_row == owner_row

    def owned(value):
        part = lax.dynamic_slice_in_dim(value, local_slot * TILE, TILE, 0)
        return jnp.where(mine, part, jnp.zeros_like(part))

    pivot_right, pivot_left = lax.psum((owned(earlier_right_factors), owned(left_u)), "row")
    pivot_panel = lax.psum_scatter(owned(panel_tiles), "row", scatter_dimension=0, tiled=True)

    share = TILE // row_devices
    my_left = lax.dynamic_slice_in_dim(pivot_left, my_row * share, share, 0)
    pivot_small = left_factors(pivot_right, pivot_right, my_left)
    contract = (((1,), (1,)), ((), ()))
    pivot_terms = lax.dot_general(pivot_small, pivot_left, contract, preferred_element_type=F32)
    diagonal = lax.psum_scatter(
        place(pivot_panel, TILE, my_col * col_width) - pivot_terms, "col", scatter_dimension=0, tiled=True
    )
    diagonal = lax.all_gather(diagonal, ("row", "col"), axis=0, tiled=True)

    left_small = left_factors(earlier_right_factors, pivot_right, left_u)
    update_terms = lax.dot_general(left_small, pivot_left, contract, preferred_element_type=F32)
    partial = place(panel_tiles, TILE, my_col * col_width) - update_terms
    updated = lax.psum_scatter(partial, "col", scatter_dimension=0, tiled=True)

    chol, inverse = factor((diagonal + diagonal.T) * 0.5)
    solved = lax.dot_general(updated, inverse, contract, precision=HI, preferred_element_type=F32)
    held = updated.shape[0]
    first = my_col * held
    chosen = jnp.logical_and(mine, first // TILE == local_slot)
    chol_rows = lax.dynamic_slice_in_dim(chol, first % TILE, held, 0)
    solved = jnp.where(chosen, chol_rows, solved)
    return lax.all_to_all(solved, "col", split_axis=1, concat_axis=0, tiled=True)


def solution(mesh):
    in_specs = (P("row", "col"), P("row", "col"), P("row", "col"), P())
    return jax.shard_map(
        functools.partial(local, mesh), mesh=mesh, in_specs=in_specs, out_specs=P("row", "col"), check_vma=False
    )
```

```python
import functools

import jax
import jax.numpy as jnp
from jax import lax
from jax.experimental import pallas as pl
from jax.experimental.pallas import tpu as pltpu
from jax.sharding import PartitionSpec as P

TILE = 1024
RANK = 256

BLK = 128
SUB = 8
F32 = jnp.float32
HI = lax.Precision.HIGHEST


def dot(a, b, dims=((1,), (0,))):
    return lax.dot_general(a, b, (dims, ((), ())), precision=HI, preferred_element_type=F32)


def eliminate(block):
    shape = (SUB, BLK)
    groups = [block[g * SUB:(g + 1) * SUB, :] for g in range(BLK // SUB)]
    lane = lax.broadcasted_iota(jnp.int32, shape, 1)
    sub = lax.broadcasted_iota(jnp.int32, shape, 0)
    for g in range(len(groups)):
        base = g * SUB
        rows = groups[g]
        cols = [jnp.broadcast_to(rows[:, base + j:base + j + 1], shape) for j in range(SUB)]
        out = rows
        for s in range(SUB):
            raw = jnp.broadcast_to(rows[s:s + 1, :], shape)
            here = lane == base + s
            mine = sub == s
            out = jnp.where(mine, raw, out)
            inverse = 1.0 / jnp.broadcast_to(cols[s][s:s + 1, :], shape)
            factor = jnp.where(mine, 0.0, cols[s] * inverse)
            unit = jnp.where(here, 1.0, raw)
            kept = jnp.where(here, 0.0, rows)
            rows = jnp.where(mine, unit * inverse, kept - factor * unit)
            for j in range(s + 1, SUB):
                head = jnp.broadcast_to(cols[j][s:s + 1, :], shape)
                cols[j] = jnp.where(mine, head * inverse, cols[j] - factor * head)
        groups[g] = out
        if g + 1 == len(groups):
            break
        reduced = [jnp.broadcast_to(rows[s:s + 1, :], shape) for s in range(SUB)]
        inside = jnp.logical_and(lane >= base, lane < base + SUB)
        for h in range(g + 1, len(groups)):
            old = groups[h]
            terms = [
                jnp.broadcast_to(old[:, base + s:base + s + 1], shape) * reduced[s] for s in range(SUB)
            ]
            while len(terms) > 1:
                terms = [terms[i] + terms[i + 1] for i in range(0, len(terms), 2)]
            groups[h] = jnp.where(inside, 0.0, old) - terms[0]
    return jnp.concatenate(groups, axis=0)


def factor_kernel(a_ref, l_ref, x_ref, w_ref):
    size = a_ref.shape[0]
    count = size // BLK
    row_id = lax.broadcasted_iota(jnp.int32, (BLK, BLK), 0)
    col_id = lax.broadcasted_iota(jnp.int32, (BLK, BLK), 1)

    @pl.loop(0, count)
    def _(i):
        at = pl.ds(pl.multiple_of(i * BLK, BLK), BLK)
        w_ref[at, :] = a_ref[at, :]
        l_ref[at, :] = jnp.zeros((BLK, size), F32)

    @pl.loop(0, count)
    def _(k):
        at = pl.ds(pl.multiple_of(k * BLK, BLK), BLK)
        done = eliminate(w_ref[at, at])
        pivots = jnp.sum(jnp.where(row_id == col_id, done, 0.0), axis=1, keepdims=True)
        scale = 1.0 / jnp.sqrt(pivots)
        upper = jnp.where(col_id >= row_id, done * scale, 0.0)
        inner = jnp.where(col_id < row_id, done * scale, 0.0) + jnp.where(row_id == col_id, scale, 0.0)
        l_ref[at, at] = upper.T
        row = dot(inner, w_ref[at, :])
        block_id = lax.broadcasted_iota(jnp.int32, (BLK, size), 1) // BLK
        row = jnp.where(block_id == k, jnp.concatenate([inner] * count, axis=1), row)
        x_ref[at, :] = jnp.where(block_id <= k, row, 0.0)
        inner_t = inner.T

        @pl.loop(k + 1, count)
        def _(i):
            there = pl.ds(pl.multiple_of(i * BLK, BLK), BLK)
            left = dot(w_ref[there, at], inner_t)
            l_ref[there, at] = left
            w_ref[there, at] = jnp.zeros((BLK, BLK), F32)
            w_ref[there, :] = w_ref[there, :] - dot(left, row)


def factor(a):
    size = a.shape[0]
    shape = jax.ShapeDtypeStruct((size, size), F32)
    return pl.pallas_call(
        factor_kernel,
        out_shape=(shape, shape),
        in_specs=[pl.BlockSpec(memory_space=pltpu.VMEM)],
        out_specs=(pl.BlockSpec(memory_space=pltpu.VMEM),) * 2,
        scratch_shapes=[pltpu.VMEM((size, size), F32)],
        compiler_params=pltpu.CompilerParams(vmem_limit_bytes=32 * 1024 * 1024),
        cost_estimate=pl.CostEstimate(flops=60_000_000_000, bytes_accessed=3 * size * size * 4, transcendentals=0),
        name="factor",
    )(a)


def left_kernel(v_ref, pivot_ref, u_ref, out_ref):
    inner = lax.dot_general(
        v_ref[...], pivot_ref[...], (((0,), (0,)), ((), ())), preferred_element_type=F32
    ).astype(jnp.bfloat16)
    out_ref[...] = jnp.dot(u_ref[...], inner, preferred_element_type=F32).astype(jnp.bfloat16)


def left_factors(v, pivot_v, u):
    slots = v.shape[0] // TILE
    rows = u.shape[0] // slots
    return pl.pallas_call(
        left_kernel,
        grid=(v.shape[1] // RANK, slots),
        out_shape=jax.ShapeDtypeStruct(u.shape, jnp.bfloat16),
        in_specs=[
            pl.BlockSpec((TILE, RANK), lambda j, t: (t, j)),
            pl.BlockSpec((TILE, RANK), lambda j, t: (0, j)),
            pl.BlockSpec((rows, RANK), lambda j, t: (t, j)),
        ],
        out_specs=pl.BlockSpec((rows, RANK), lambda j, t: (t, j)),
        cost_estimate=pl.CostEstimate(
            flops=2 * v.size * RANK + 2 * u.size * RANK,
            bytes_accessed=2 * (v.size + 2 * u.size + pivot_v.size),
            transcendentals=0,
        ),
        name="left",
    )(v, pivot_v, u)


MESH = pl.DeviceIdType.MESH


def exchange_kernel(depth, chips, part_ref, out_ref, got, sends, recvs, pair_send, pair_recv):
    me = lax.axis_index("row")
    col = lax.axis_index("col")
    chip, core = me // 2, me % 2
    share = part_ref.shape[0]
    sub = share // depth
    pair = chip * 2 + 1 - core
    cols = [(col + d) % depth for d in range(1, depth)]
    peers = [((chip + d) % chips) * 2 + core for d in range(1, chips)]

    barrier = pltpu.get_barrier_semaphore()
    for other in cols:
        pl.semaphore_signal(barrier, inc=1, device_id=(me, other), device_id_type=MESH)
    for other in peers + [pair]:
        pl.semaphore_signal(barrier, inc=1, device_id=(other, col), device_id_type=MESH)
    pl.semaphore_wait(barrier, depth + chips - 1)

    def copy(src, dst, i, target):
        return pltpu.make_async_remote_copy(
            src_ref=src, dst_ref=dst, send_sem=sends.at[i], recv_sem=recvs.at[i],
            device_id=target, device_id_type=MESH,
        )

    first = []
    for d, other in enumerate(cols):
        rows = pl.ds(pl.multiple_of(other * sub, sub), sub)
        first.append(copy(part_ref.at[rows, :], got.at[d], d, (me, other)))
        first[-1].start()
    total = part_ref[pl.ds(pl.multiple_of(col * sub, sub), sub), :]
    for d, item in enumerate(first):
        item.wait_recv()
        total = total + got[d]
    mine = pl.ds(pl.multiple_of(me * share + col * sub, sub), sub)
    out_ref[mine, :] = total

    second = []
    for d, other in enumerate(cols):
        second.append(copy(out_ref.at[mine, :], out_ref.at[mine, :], depth - 1 + d, (me, other)))
        second[-1].start()
    for item in second:
        item.wait_recv()

    block = out_ref.at[pl.ds(pl.multiple_of(me * share, share), share), :]
    third = []
    for d, other in enumerate(peers):
        third.append(copy(block, block, 2 * (depth - 1) + d, (other, col)))
        third[-1].start()
    fourth = []
    for d in range(chips):
        if d:
            third[d - 1].wait_recv()
        owner = ((chip + chips - d) % chips) * 2 + core
        held = out_ref.at[pl.ds(pl.multiple_of(owner * share, share), share), :]
        fourth.append(
            pltpu.make_async_remote_copy(
                src_ref=held, dst_ref=held, send_sem=pair_send.at[d], recv_sem=pair_recv.at[d],
                device_id=(pair, col), device_id_type=MESH,
            )
        )
        fourth[-1].start()
    for item in fourth:
        item.wait_recv()
    for item in first + second + third + fourth:
        item.wait_send()


def exchange(mesh, part):
    row_devices, depth = mesh.shape["row"], mesh.shape["col"]
    chips = row_devices // 2
    share, width = part.shape
    links = 2 * (depth - 1) + chips - 1
    return pl.pallas_call(
        functools.partial(exchange_kernel, depth, chips),
        out_shape=jax.ShapeDtypeStruct((share * row_devices, width), F32),
        in_specs=[pl.BlockSpec(memory_space=pltpu.VMEM)],
        out_specs=pl.BlockSpec(memory_space=pltpu.VMEM),
        scratch_shapes=[
            pltpu.VMEM((depth - 1, share // depth, width), F32),
            pltpu.SemaphoreType.DMA((links,)),
            pltpu.SemaphoreType.DMA((links,)),
            pltpu.SemaphoreType.DMA((chips,)),
            pltpu.SemaphoreType.DMA((chips,)),
        ],
        compiler_params=pltpu.CompilerParams(collective_id=0, has_side_effects=True),
        cost_estimate=pl.CostEstimate(flops=40_000_000_000, bytes_accessed=share * row_devices * width * 8, transcendentals=0),
        name="exchange",
    )(part)


def place(block, width, start):
    return lax.dynamic_update_slice_in_dim(jnp.zeros((block.shape[0], width), block.dtype), block, start, 1)


def local(mesh, panel_tiles, left_u, earlier_right_factors, tile_global_index):
    row_devices = mesh.shape["row"]
    tile_count = tile_global_index.shape[0]
    rows, col_width = panel_tiles.shape
    slots = rows // TILE
    pivot_position = jnp.sum(
        jnp.where(tile_global_index == 0, jnp.arange(tile_count, dtype=jnp.int32), 0)
    )
    owner_row = pivot_position // slots
    local_slot = pivot_position % slots
    my_row = lax.axis_index("row")
    my_col = lax.axis_index("col")
    mine = my_row == owner_row

    def owned(value):
        part = lax.dynamic_slice_in_dim(value, local_slot * TILE, TILE, 0)
        return jnp.where(mine, part, jnp.zeros_like(part))

    pivot_right, pivot_left = lax.psum((owned(earlier_right_factors), owned(left_u)), "row")
    pivot_panel, pivot_right, pivot_left = lax.optimization_barrier(
        (owned(panel_tiles), pivot_right, pivot_left)
    )
    pivot_panel = lax.psum_scatter(pivot_panel, "row", scatter_dimension=0, tiled=True)

    share = TILE // row_devices
    my_left = lax.dynamic_slice_in_dim(pivot_left, my_row * share, share, 0)
    pivot_small = left_factors(pivot_right, pivot_right, my_left)
    contract = (((1,), (1,)), ((), ()))
    pivot_terms = lax.dot_general(pivot_small, pivot_left, contract, preferred_element_type=F32)
    diagonal = place(pivot_panel, TILE, my_col * col_width) - pivot_terms

    left_small = left_factors(earlier_right_factors, pivot_right, left_u)
    update_terms = lax.dot_general(left_small, pivot_left, contract, preferred_element_type=F32)
    partial = place(panel_tiles, TILE, my_col * col_width) - update_terms
    partial, diagonal = lax.optimization_barrier((partial, diagonal))
    diagonal = exchange(mesh, diagonal)
    updated = lax.psum_scatter(partial, "col", scatter_dimension=0, tiled=True)

    chol, inverse = factor((diagonal + diagonal.T) * 0.5)
    solved = lax.dot_general(updated, inverse, contract, precision=HI, preferred_element_type=F32)
    held = updated.shape[0]
    first = my_col * held
    chosen = jnp.logical_and(mine, first // TILE == local_slot)
    chol_rows = lax.dynamic_slice_in_dim(chol, first % TILE, held, 0)
    solved = jnp.where(chosen, chol_rows, solved)
    return lax.all_to_all(solved, "col", split_axis=1, concat_axis=0, tiled=True)


def solution(mesh):
    in_specs = (P("row", "col"), P("row", "col"), P("row", "col"), P())
    return jax.shard_map(
        functools.partial(local, mesh), mesh=mesh, in_specs=in_specs, out_specs=P("row", "col"), check_vma=False
    )
```
